32 devices in a mesh: wide: 16 (over z, x, core), narrow: 2 (over y).
Axes of the slice: x: 2, y: 2, z: 4, core: 2. Of those that a mesh axis runs over, the one named last changes fastest.
Arguments:
- activations: float32 [1024, 17408], P('wide', 'narrow'), may hold values from -6 to 6
- act_basis: float32 [17408, 17408], P('narrow', 'wide'), may hold values from -0.046875 to 0.046875
- grads: float32 [1024, 5120], P(None, 'wide'), may hold values from -0.3 to 0.3
- grad_basis: float32 [5120, 5120], P('wide', 'narrow'), may hold values from -0.078125 to 0.078125
- seq_ids: int32 [1024], replicated, may hold values from 0 to 3, never falling along the last dimension, each value on 1 to 512 neighbouring positions
Outputs:
- eigenvalues: float32 [17408, 5120], P('wide', 'narrow')
The draws below stay inside these ranges and needn't reach their ends.
Inputs may be any that keep to these rules, and one draw needn't show every extreme that they name: `seq_ids`: never falling along the rows; every sequence has at least one row and at most 512 rows, and one sequence has exactly 512.
All inputs are finite; a program needn't handle non-finite values.
Results may differ from the reference program's by a relative error of at most 0.0003.
Values sent between devices are 32-bit elements; how exact they have to be, the bound alone decides.
A program may use at most 192 MiB of HBM per device.

```python
import math
import jax
import jax.numpy as jnp
import numpy as np
from jax import lax

D_IN = 17408
D_OUT = 5120
ROWS = 1024
SEQS = 4
SEQ_MOST = 512


def levels(stream_key, extent, split, smallest, high):
    level, own = 1.0, jax.random.fold_in(stream_key, 6)
    for position, blocks in split:
        steps = jnp.exp(jax.random.uniform(jax.random.fold_in(own, position), (blocks,), jnp.float32, smallest / len(split), high / len(split)))
        level = level * jnp.repeat(steps, extent[position] // blocks).reshape([-1 if axis == position else 1 for axis in range(len(extent))])
    return level


def profile(number_of, total, most, slope):
    portions = [(1 << 20) // math.isqrt(standing ** slope) + 1 for standing in range(2, number_of + 1)]
    surplus, given = total - most - (number_of - 1), [1] * (number_of - 1)
    while surplus > 0:
        free = [i for i in range(number_of - 1) if given[i] < most]
        pool, remaining = sum([portions[i] for i in free]), surplus
        for i in free:
            addition = min(most - given[i], max(1, remaining * portions[i] // pool), surplus)
            given[i] = given[i] + addition
            surplus = surplus - addition
    return np.array([most] + given)


def uneven_parts(rng, number_of, total, bound, slope):
    if number_of == 2:
        one = jax.random.randint(rng, (), max(1, total - bound), min(bound, total - 1) + 1)
        return jnp.stack([one, total - one])
    lengths = jnp.asarray(profile(number_of, total, bound, slope), jnp.int32)
    couples = (number_of - 1) // 2
    source_of, sink = lengths[1:1 + 2 * couples:2], lengths[2:2 + 2 * couples:2]
    slack = jnp.minimum(source_of - 1, bound - sink)
    moved = jax.random.randint(jax.random.fold_in(rng, 1), (couples,), 0, 1 << 20) % (slack + 1)
    lengths = lengths.at[1:1 + 2 * couples:2].set(source_of - moved).at[2:2 + 2 * couples:2].set(sink + moved)
    return lengths[jax.random.permutation(jax.random.fold_in(rng, 2), number_of)]


def centred(key, extent, width, limit, pieces=(), kind=jnp.bfloat16):
    array = width * jax.random.normal(key, extent, jnp.float32)
    if pieces:
        array = array * levels(key, extent, pieces, -0.22, 0.18)
    return jnp.clip(array, -limit, limit).astype(kind)


def setup_inputs(seed: int = 0) -> dict:
    arg_keys = jax.random.split(jax.random.key(seed), 6)
    activations = centred(arg_keys[0], (ROWS, D_IN), 1.0, 6.0, ((0, 16), (1, 2)), jnp.float32)
    act_basis = centred(arg_keys[1], (D_IN, D_IN), D_IN ** -0.5, 0.046875, ((0, 2), (1, 16)), jnp.float32)
    grads = centred(arg_keys[2], (ROWS, D_OUT), 0.05, 0.3, ((1, 16),), jnp.float32)
    grad_basis = centred(arg_keys[3], (D_OUT, D_OUT), D_OUT ** -0.5, 0.078125, ((0, 16), (1, 2)), jnp.float32)
    seq_ids = jnp.searchsorted(jnp.cumsum(uneven_parts(arg_keys[4], SEQS, ROWS, SEQ_MOST, 0)), jnp.arange(ROWS), side="right").astype(jnp.int32)
    return dict(activations=activations, act_basis=act_basis, grads=grads, grad_basis=grad_basis, seq_ids=seq_ids)


def reference(activations, act_basis, grads, grad_basis, seq_ids):
    highest = lax.Precision.HIGHEST
    rotated_acts = jnp.dot(activations, act_basis, precision=highest, preferred_element_type=jnp.float32)
    rotated_grads = jnp.dot(grads, grad_basis, precision=highest, preferred_element_type=jnp.float32)

    def accumulate(running, seq_label):
        seq_mask = (seq_ids == seq_label).astype(jnp.float32)[:, None]
        moment = jnp.dot(rotated_acts.T, rotated_grads * seq_mask, precision=highest, preferred_element_type=jnp.float32)
        return running + moment * moment, None

    running = jnp.zeros((rotated_acts.shape[1], rotated_grads.shape[1]), jnp.float32)
    running, unused = lax.scan(accumulate, running, jnp.arange(SEQS, dtype=jnp.int32))
    return running / jnp.float32(SEQS)
```

```python
import functools

import jax
import jax.numpy as jnp
from jax import lax
from jax.experimental import pallas as pl
from jax.experimental.pallas import tpu as pltpu
from jax.sharding import PartitionSpec as P

SEQS = 4
SEQ_MOST = 512
MESH = pl.DeviceIdType.MESH


def dot(a, b):
    return jnp.dot(a, b, precision=lax.Precision.HIGH, preferred_element_type=jnp.float32)


def split(value):
    high = value.astype(jnp.bfloat16)
    return high, (value - high.astype(jnp.float32)).astype(jnp.bfloat16)


def three_pass(a, b):
    a_high, a_low = split(a)
    b_high, b_low = split(b)
    contract = (((1,), (1,)), ((), ()))
    mul = functools.partial(lax.dot_general, dimension_numbers=contract, preferred_element_type=jnp.float32)
    return mul(a_high, b_high) + (mul(a_high, b_low) + mul(a_low, b_high))


def depth_tile(depth):
    best = 128
    for tile in range(128, min(depth, 1024) + 1, 128):
        if depth % tile == 0:
            best = tile
    return best


def gather_kernel(line_size, swap, x_ref, u_ref, gathered, part, other, own, acc,
                  send_line, send_pair, send_core, recv, own_sem, out_sem, send_swap, recv_swap):
    rows, depth = x_ref.shape
    group = 4 * rows
    me = lax.axis_index("wide")
    side = lax.axis_index("narrow")
    line, pair, core = me // 4, (me // 2) % 2, me % 2

    def index(l, p, c):
        return (l * 2 + p) * 2 + c

    def wide_id(w):
        return (w, side)

    pair_id = wide_id(index(line, 1 - pair, core))
    core_id = wide_id(index(line, pair, 1 - core))
    left, right = line - 1, line + 1
    has_left, has_right = line > 0, line < line_size - 1

    barrier = pltpu.get_barrier_semaphore()
    pl.semaphore_signal(barrier, inc=1, device_id=pair_id, device_id_type=MESH)
    pl.semaphore_signal(barrier, inc=1, device_id=core_id, device_id_type=MESH)
    if swap:
        pl.semaphore_signal(barrier, inc=1, device_id=(me, 1 - side), device_id_type=MESH)

    @pl.when(has_left)
    def _():
        pl.semaphore_signal(barrier, inc=1, device_id=wide_id(index(left, pair, core)), device_id_type=MESH)

    @pl.when(has_right)
    def _():
        pl.semaphore_signal(barrier, inc=1, device_id=wide_id(index(right, pair, core)), device_id_type=MESH)

    pl.semaphore_wait(
        barrier, (3 if swap else 2) + jnp.minimum(line, 1) + jnp.minimum(line_size - 1 - line, 1)
    )

    def block(w):
        return gathered.at[pl.ds(pl.multiple_of(w * rows, 8), rows), :]

    def send(src, w, sem, target):
        return pltpu.make_async_remote_copy(
            src_ref=src, dst_ref=block(w), send_sem=sem, recv_sem=recv.at[w],
            device_id=target, device_id_type=MESH)

    def line_send(src, l, step):
        return send(src, index(l, pair, core), send_line.at[l],
                    wide_id(index(line + step, pair, core)))

    def pair_send(src, l):
        return send(src, index(l, pair, core), send_pair.at[l], pair_id)

    def core_send(src, l, p):
        return send(src, index(l, p, core), send_core.at[index(l, p, 0) // 2], core_id)

    def wait_block(w):
        pltpu.make_async_copy(block(w), block(w), recv.at[w]).wait()

    own_left = send(x_ref, me, send_line.at[line_size], wide_id(index(left, pair, core)))
    own_right = send(x_ref, me, send_line.at[line], wide_id(index(right, pair, core)))

    @pl.when(has_right)
    def _():
        own_right.start()

    @pl.when(has_left)
    def _():
        own_left.start()

    pair_send(x_ref, line).start()
    core_send(x_ref, line, pair).start()
    load = pltpu.make_async_copy(x_ref, own, own_sem.at[0])
    load.start()
    load.wait()
    store = pltpu.make_async_copy(own, block(me), own_sem.at[1])
    store.start()
    store.wait()

    tile = depth_tile(depth)

    def group_rows(ref, l):
        return ref.at[pl.ds(pl.multiple_of(l * group, 8), group), :]

    def swap_copy(l):
        return pltpu.make_async_remote_copy(
            src_ref=group_rows(part, l), dst_ref=group_rows(other, l),
            send_sem=send_swap.at[l], recv_sem=recv_swap.at[l],
            device_id=(me, 1 - side), device_id_type=MESH)

    def arrive(l, step):
        w = index(l, pair, core)
        wait_block(w)

        @pl.when((line + step >= 0) & (line + step < line_size))
        def _():
            line_send(block(w), l, step).start()

        pair_send(block(w), l).start()
        core_send(block(w), l, pair).start()

    def finish(l):
        crossed = index(l, 1 - pair, core)
        wait_block(crossed)
        core_send(block(crossed), l, 1 - pair).start()
        wait_block(index(l, pair, 1 - core))
        wait_block(index(l, 1 - pair, 1 - core))
        acc[...] = jnp.zeros_like(acc)

        def body(x_tile, u_tile):
            acc[...] += three_pass(x_tile[...], u_tile[...])

        pltpu.emit_pipeline(
            body,
            grid=(depth // tile,),
            in_specs=[
                pl.BlockSpec((group, tile), lambda k: (0, k)),
                pl.BlockSpec((u_ref.shape[0], tile), lambda k: (0, k)),
            ],
        )(group_rows(gathered, l), u_ref)
        out = pltpu.make_async_copy(acc, group_rows(part, l), out_sem)
        out.start()
        out.wait()
        if swap:
            swap_copy(l).start()

    def step(d, carry):
        @pl.when((d < line_size) & (line - d >= 0))
        def _():
            arrive(line - d, 1)

        @pl.when((d < line_size) & (line + d < line_size))
        def _():
            arrive(line + d, -1)

        @pl.when(line - (d - 1) >= 0)
        def _():
            finish(line - (d - 1))

        @pl.when((d > 1) & (line + (d - 1) < line_size))
        def _():
            finish(line + (d - 1))

        return carry

    lax.fori_loop(1, line_size + 1, step, 0)

    def drain(l, carry):
        @pl.when((l <= line) & has_right)
        def _():
            line_send(block(index(l, pair, core)), l, 1).wait_send()

        @pl.when((l > line) & has_left)
        def _():
            line_send(block(index(l, pair, core)), l, -1).wait_send()

        pair_send(block(index(l, pair, core)), l).wait_send()
        core_send(block(index(l, 0, core)), l, 0).wait_send()
        core_send(block(index(l, 1, core)), l, 1).wait_send()
        if swap:
            swap_copy(l).wait()
        return carry

    lax.fori_loop(0, line_size, drain, 0)

    @pl.when(has_left)
    def _():
        own_left.wait_send()


def gather_product(wide, narrow, activations, act_basis):
    rows, depth = activations.shape
    cols = act_basis.shape[1]
    line_size = wide // 4
    swap = narrow == 2
    full = wide * rows
    shape = functools.partial(jax.ShapeDtypeStruct, dtype=jnp.float32)
    hbm = pl.BlockSpec(memory_space=pltpu.HBM)
    gathered, part, other = pl.pallas_call(
        functools.partial(gather_kernel, line_size, swap),
        out_shape=[shape((full, depth)), shape((full, cols)), shape((full, cols))],
        in_specs=[hbm, hbm],
        out_specs=[hbm, hbm, hbm],
        scratch_shapes=[
            pltpu.VMEM((rows, depth), jnp.float32),
            pltpu.VMEM((4 * rows, cols), jnp.float32),
            pltpu.SemaphoreType.DMA((line_size + 1,)),
            pltpu.SemaphoreType.DMA((line_size,)),
            pltpu.SemaphoreType.DMA((2 * line_size,)),
            pltpu.SemaphoreType.DMA((wide,)),
            pltpu.SemaphoreType.DMA((2,)),
            pltpu.SemaphoreType.DMA,
            pltpu.SemaphoreType.DMA((line_size,)),
            pltpu.SemaphoreType.DMA((line_size,)),
        ],
        cost_estimate=pl.CostEstimate(
            flops=6 * full * depth * cols, bytes_accessed=4 * line_size * depth * cols, transcendentals=0),
        compiler_params=pltpu.CompilerParams(
            collective_id=0, has_side_effects=True, vmem_limit_bytes=48 * 1024 * 1024),
    )(activations, act_basis.T)
    return part + other if swap else lax.psum(part, "narrow")


def per_device(wide, narrow, activations, act_basis, grads, grad_basis, seq_ids):
    rotated_grads = lax.psum(dot(grads, grad_basis), "wide")
    rotated_acts = gather_product(wide, narrow, activations, act_basis)
    token_rows = rotated_grads.shape[0]
    running = None
    for seq_label in range(SEQS):
        first_row = jnp.sum((seq_ids < seq_label).astype(jnp.int32))
        start = jnp.minimum(first_row, token_rows - SEQ_MOST)
        ids_window = lax.dynamic_slice_in_dim(seq_ids, start, SEQ_MOST, 0)
        mask = (ids_window == seq_label).astype(jnp.float32)[:, None]
        acts_window = lax.dynamic_slice_in_dim(rotated_acts, start, SEQ_MOST, 0)
        grads_window = lax.dynamic_slice_in_dim(rotated_grads, start, SEQ_MOST, 0) * mask
        moment = dot(acts_window.T, grads_window)
        running = moment * moment if running is None else running + moment * moment
    return running / jnp.float32(SEQS)


def solution(mesh):
    wide, narrow = mesh.shape["wide"], mesh.shape["narrow"]

    def body(*args):
        return per_device(wide, narrow, *args)

    in_specs = (P("wide", "narrow"), P("narrow", "wide"), P(None, "wide"), P("wide", "narrow"), P())
    return jax.shard_map(
        body, mesh=mesh, in_specs=in_specs, out_specs=P("wide", "narrow"), check_vma=False
    )
```

```python
import functools

import jax
import jax.numpy as jnp
from jax import lax
from jax.experimental import pallas as pl
from jax.experimental.pallas import tpu as pltpu
from jax.sharding import PartitionSpec as P

SEQS = 4
SEQ_MOST = 512
MESH = pl.DeviceIdType.MESH


def dot(a, b):
    return jnp.dot(a, b, precision=lax.Precision.HIGH, preferred_element_type=jnp.float32)


def split(value):
    high = value.astype(jnp.bfloat16)
    return high, (value - high.astype(jnp.float32)).astype(jnp.bfloat16)


def three_pass(a, b):
    a_high, a_low = split(a)
    b_high, b_low = split(b)
    contract = (((1,), (1,)), ((), ()))
    mul = functools.partial(lax.dot_general, dimension_numbers=contract, preferred_element_type=jnp.float32)
    return mul(a_high, b_high) + (mul(a_high, b_low) + mul(a_low, b_high))


def depth_tile(depth):
    best = 128
    for tile in range(128, min(depth, 1024) + 1, 128):
        if depth % tile == 0:
            best = tile
    return best


def gather_kernel(line_size, swap, x_ref, u_ref, gathered, part, other, own, acc,
                  send_line, send_pair, send_core, recv, own_sem, out_sem, send_swap, recv_swap):
    rows, depth = x_ref.shape
    group = 4 * rows
    me = lax.axis_index("wide")
    side = lax.axis_index("narrow")
    line, pair, core = me // 4, (me // 2) % 2, me % 2

    def index(l, p, c):
        return (l * 2 + p) * 2 + c

    def wide_id(w):
        return (w, side)

    pair_id = wide_id(index(line, 1 - pair, core))
    core_id = wide_id(index(line, pair, 1 - core))
    left, right = line - 1, line + 1
    has_left, has_right = line > 0, line < line_size - 1

    barrier = pltpu.get_barrier_semaphore()
    pl.semaphore_signal(barrier, inc=1, device_id=pair_id, device_id_type=MESH)
    pl.semaphore_signal(barrier, inc=1, device_id=core_id, device_id_type=MESH)
    if swap:
        pl.semaphore_signal(barrier, inc=1, device_id=(me, 1 - side), device_id_type=MESH)

    @pl.when(has_left)
    def _():
        pl.semaphore_signal(barrier, inc=1, device_id=wide_id(index(left, pair, core)), device_id_type=MESH)

    @pl.when(has_right)
    def _():
        pl.semaphore_signal(barrier, inc=1, device_id=wide_id(index(right, pair, core)), device_id_type=MESH)

    pl.semaphore_wait(
        barrier, (3 if swap else 2) + jnp.minimum(line, 1) + jnp.minimum(line_size - 1 - line, 1)
    )

    def block(w):
        return gathered.at[pl.ds(pl.multiple_of(w * rows, 8), rows), :]

    def send(src, w, sem, target):
        return pltpu.make_async_remote_copy(
            src_ref=src, dst_ref=block(w), send_sem=sem, recv_sem=recv.at[w],
            device_id=target, device_id_type=MESH)

    def line_send(src, l, step):
        return send(src, index(l, pair, core), send_line.at[l],
                    wide_id(index(line + step, pair, core)))

    def pair_send(src, l):
        return send(src, index(l, pair, core), send_pair.at[l], pair_id)

    def core_send(src, l, p):
        return send(src, index(l, p, core), send_core.at[index(l, p, 0) // 2], core_id)

    def wait_block(w):
        pltpu.make_async_copy(block(w), block(w), recv.at[w]).wait()

    own_left = send(x_ref, me, send_line.at[line_size], wide_id(index(left, pair, core)))
    own_right = send(x_ref, me, send_line.at[line], wide_id(index(right, pair, core)))

    @pl.when(has_right)
    def _():
        own_right.start()

    @pl.when(has_left)
    def _():
        own_left.start()

    pair_send(x_ref, line).start()
    core_send(x_ref, line, pair).start()
    load = pltpu.make_async_copy(x_ref, own, own_sem.at[0])
    load.start()
    load.wait()
    store = pltpu.make_async_copy(own, block(me), own_sem.at[1])
    store.start()
    store.wait()

    tile = depth_tile(depth)

    def group_rows(ref, l):
        return ref.at[pl.ds(pl.multiple_of(l * group, 8), group), :]

    def swap_copy(l):
        return pltpu.make_async_remote_copy(
            src_ref=group_rows(part, l), dst_ref=group_rows(other, l),
            send_sem=send_swap.at[l], recv_sem=recv_swap.at[l],
            device_id=(me, 1 - side), device_id_type=MESH)

    def arrive(l, step):
        w = index(l, pair, core)
        wait_block(w)

        @pl.when((line + step >= 0) & (line + step < line_size))
        def _():
            line_send(block(w), l, step).start()

        pair_send(block(w), l).start()
        core_send(block(w), l, pair).start()

    def finish(l):
        crossed = index(l, 1 - pair, core)
        wait_block(crossed)
        core_send(block(crossed), l, 1 - pair).start()
        wait_block(index(l, pair, 1 - core))
        wait_block(index(l, 1 - pair, 1 - core))
        acc[...] = jnp.zeros_like(acc)

        def body(x_tile, u_tile):
            acc[...] += three_pass(x_tile[...], u_tile[...])

        pltpu.emit_pipeline(
            body,
            grid=(depth // tile,),
            in_specs=[
                pl.BlockSpec((group, tile), lambda k: (0, k)),
                pl.BlockSpec((u_ref.shape[0], tile), lambda k: (0, k)),
            ],
        )(group_rows(gathered, l), u_ref)
        out = pltpu.make_async_copy(acc, group_rows(part, l), out_sem)
        out.start()
        out.wait()
        if swap:
            swap_copy(l).start()

    def step(d, carry):
        @pl.when((d < line_size) & (line - d >= 0))
        def _():
            arrive(line - d, 1)

        @pl.when((d < line_size) & (line + d < line_size))
        def _():
            arrive(line + d, -1)

        @pl.when(line - (d - 1) >= 0)
        def _():
            finish(line - (d - 1))

        @pl.when((d > 1) & (line + (d - 1) < line_size))
        def _():
            finish(line + (d - 1))

        return carry

    lax.fori_loop(1, line_size + 1, step, 0)

    def drain(l, carry):
        @pl.when((l <= line) & has_right)
        def _():
            line_send(block(index(l, pair, core)), l, 1).wait_send()

        @pl.when((l > line) & has_left)
        def _():
            line_send(block(index(l, pair, core)), l, -1).wait_send()

        pair_send(block(index(l, pair, core)), l).wait_send()
        core_send(block(index(l, 0, core)), l, 0).wait_send()
        core_send(block(index(l, 1, core)), l, 1).wait_send()
        if swap:
            swap_copy(l).wait()
        return carry

    lax.fori_loop(0, line_size, drain, 0)

    @pl.when(has_left)
    def _():
        own_left.wait_send()


def gather_product(wide, narrow, activations, act_basis):
    rows, depth = activations.shape
    cols = act_basis.shape[1]
    line_size = wide // 4
    swap = narrow == 2
    full = wide * rows
    shape = functools.partial(jax.ShapeDtypeStruct, dtype=jnp.float32)
    hbm = pl.BlockSpec(memory_space=pltpu.HBM)
    gathered, part, other = pl.pallas_call(
        functools.partial(gather_kernel, line_size, swap),
        out_shape=[shape((full, depth)), shape((full, cols)), shape((full, cols))],
        in_specs=[hbm, hbm],
        out_specs=[hbm, hbm, hbm],
        scratch_shapes=[
            pltpu.VMEM((rows, depth), jnp.float32),
            pltpu.VMEM((4 * rows, cols), jnp.float32),
            pltpu.SemaphoreType.DMA((line_size + 1,)),
            pltpu.SemaphoreType.DMA((line_size,)),
            pltpu.SemaphoreType.DMA((2 * line_size,)),
            pltpu.SemaphoreType.DMA((wide,)),
            pltpu.SemaphoreType.DMA((2,)),
            pltpu.SemaphoreType.DMA,
            pltpu.SemaphoreType.DMA((line_size,)),
            pltpu.SemaphoreType.DMA((line_size,)),
        ],
        cost_estimate=pl.CostEstimate(
            flops=6 * full * depth * cols, bytes_accessed=4 * line_size * depth * cols, transcendentals=0),
        compiler_params=pltpu.CompilerParams(
            collective_id=0, has_side_effects=True, vmem_limit_bytes=48 * 1024 * 1024),
    )(activations, act_basis.T)
    return part + other if swap else lax.psum(part, "narrow")


def per_device(wide, narrow, activations, act_basis, grads, grad_basis, seq_ids):
    rotated_grads = lax.psum(dot(grads, grad_basis), "wide")
    rotated_acts = gather_product(wide, narrow, activations, act_basis)
    token_rows = rotated_grads.shape[0]
    counts = [jnp.sum((seq_ids == s).astype(jnp.int32)) for s in range(SEQS)]
    ranks = [
        sum(((counts[t] >= counts[s]) if t < s else (counts[t] > counts[s])).astype(jnp.int32)
            for t in range(SEQS) if t != s)
        for s in range(SEQS)
    ]
    running = None
    for rank in range(SEQS):
        most = SEQ_MOST if rank == 0 else (token_rows - SEQ_MOST) // rank
        window = min(SEQ_MOST, -(-most // 128) * 128)
        seq_label = sum(s * (ranks[s] == rank).astype(jnp.int32) for s in range(SEQS))
        first_row = jnp.sum((seq_ids < seq_label).astype(jnp.int32))
        start = jnp.minimum(first_row, token_rows - window)
        ids_window = lax.dynamic_slice_in_dim(seq_ids, start, window, 0)
        mask = (ids_window == seq_label).astype(jnp.float32)[:, None]
        acts_window = lax.dynamic_slice_in_dim(rotated_acts, start, window, 0)
        grads_window = lax.dynamic_slice_in_dim(rotated_grads, start, window, 0) * mask
        moment = dot(acts_window.T, grads_window)
        running = moment * moment if running is None else running + moment * moment
    return running / jnp.float32(SEQS)


def solution(mesh):
    wide, narrow = mesh.shape["wide"], mesh.shape["narrow"]

    def body(*args):
        return per_device(wide, narrow, *args)

    in_specs = (P("wide", "narrow"), P("narrow", "wide"), P(None, "wide"), P("wide", "narrow"), P())
    return jax.shard_map(
        body, mesh=mesh, in_specs=in_specs, out_specs=P("wide", "narrow"), check_vma=False
    )
```
